32 devices in a mesh: gx: 8 (over z, y), gy: 4 (over x, core).
Axes of the slice: x: 2, y: 2, z: 4, core: 2. Of those that a mesh axis runs over, the one named last changes fastest.
Arguments:
- conc_start: float32 [64, 32, 128], P('gx', 'gy'), may hold values from 0.5 to 2
- diffusion: float32 [64, 32, 128], P('gx', 'gy'), may hold values from 0.03 to 0.12
- courant: float32 [64, 32, 128], P('gx', 'gy'), may hold values from 0.05 to 0.25
- uptake: float32 [64, 32, 128], P('gx', 'gy'), may hold values from 0.02 to 0.2
- directions: float32 [32, 64, 32, 128], P(None, 'gx', 'gy'), may hold values from -6 to 6
- sensor_cell: int32 [8, 4, 64], P('gx', 'gy'), may hold values from 0 to 8191
- sensor_step: int32 [8, 4, 64], P('gx', 'gy'), may hold values from 1 to 4
Outputs:
- curvature_product: float32 [32, 64, 32, 128], P(None, 'gx', 'gy')
The draws below stay inside these ranges and needn't reach their ends.
All inputs are finite; a program needn't handle non-finite values.
Results may differ from the reference program's by a relative error of at most 0.00002.
Values sent between devices are 32-bit elements; how exact they have to be, the bound alone decides.
A program may use at most 64 MiB of HBM per device.

```python
import math
import jax
import jax.numpy as jnp
from jax import lax

CX = 8
CY = 8
LZ = 128
NDIR = 32
STEPS = 4
S_DEV = 64
NX = 64
NY = 32
N_GX = 8
N_GY = 4


def with_ends(result, own_key, low, largest):
    spot = [jax.random.randint(jax.random.fold_in(own_key, axis), (), 0, length) for axis, length in enumerate(result.shape)]
    widest = result.shape.index(max(result.shape))
    neighbour = spot[:widest] + [(spot[widest] + 1) % result.shape[widest]] + spot[widest + 1:]
    return result.at[tuple(spot)].set(low).at[tuple(neighbour)].set(largest)


def block_levels(stream_key, extent, split, least, high):
    factor_of, own = 1.0, jax.random.fold_in(stream_key, 6)
    for dim, shards_of in split:
        steps = jnp.exp(jax.random.uniform(jax.random.fold_in(own, dim), (shards_of,), jnp.float32, least / len(split), high / len(split)))
        factor_of = factor_of * jnp.repeat(steps, extent[dim] // shards_of).reshape([-1 if axis == dim else 1 for axis in range(len(extent))])
    return factor_of


def centred(own_key, extent, scale, reach, pieces=(), kind=jnp.bfloat16):
    array = jax.random.normal(own_key, extent, jnp.float32) * scale
    if len(pieces) > 0:
        array = block_levels(own_key, extent, pieces, -0.22, 0.18) * array
    return jnp.clip(array, min=-reach, max=reach).astype(kind)


def setup_inputs(seed: int = 0) -> dict:
    arg_keys = jax.random.split(jax.random.key(seed), 8)
    return {
        "conc_start": jnp.clip(0.5 + 1.5 * jax.random.uniform(arg_keys[0], (NX, NY, LZ), jnp.float32) ** block_levels(arg_keys[0], (NX, NY, LZ), ((0, 8), (1, 4)), -0.2, 0.2), 0.5, 2.0),
        "diffusion": jnp.clip(jnp.exp(math.log(0.12) - 1.3862944 * jax.random.uniform(arg_keys[1], (NX, NY, LZ), jnp.float32) ** block_levels(arg_keys[1], (NX, NY, LZ), ((0, 8), (1, 4)), -0.2, 0.2)), 0.03, 0.12),
        "courant": jnp.clip(jnp.exp(math.log(0.25) - 1.609438 * jax.random.uniform(arg_keys[2], (NX, NY, LZ), jnp.float32) ** block_levels(arg_keys[2], (NX, NY, LZ), ((0, 8), (1, 4)), -0.2, 0.2)), 0.05, 0.25),
        "uptake": jnp.clip(jnp.exp(math.log(0.2) - 2.3025851 * jax.random.uniform(arg_keys[3], (NX, NY, LZ), jnp.float32) ** block_levels(arg_keys[3], (NX, NY, LZ), ((0, 8), (1, 4)), -0.2, 0.2)), 0.02, 0.2),
        "directions": centred(arg_keys[4], (NDIR, NX, NY, LZ), 1.0, 6.0, ((1, 8), (2, 4)), jnp.float32),
        "sensor_cell": with_ends(jax.random.randint(arg_keys[5], (N_GX, N_GY, S_DEV), 0, CX * CY * LZ), jax.random.fold_in(arg_keys[5], 1), 0, (CX * CY * LZ) - 1).astype(jnp.int32),
        "sensor_step": with_ends(jax.random.randint(arg_keys[6], (N_GX, N_GY, S_DEV), 1, STEPS + 1), jax.random.fold_in(arg_keys[6], 1), 1, STEPS).astype(jnp.int32),
    }


HALF_SATURATION = 0.5
PRIOR_WEIGHT = 0.2
PRIOR_SHIFT = 0.5


def pad_sides(field):
    widths = [(0, 0)] * (field.ndim - 3) + [(1, 1), (1, 1), (0, 0)]
    return jnp.pad(field, widths)


def spread(padded):
    inner = padded[..., 1:-1, 1:-1, :]
    column = jnp.pad(inner, [(0, 0)] * (inner.ndim - 1) + [(1, 1)])
    beside = padded[..., 2:, 1:-1, :] + padded[..., :-2, 1:-1, :]
    beside = beside + padded[..., 1:-1, 2:, :] + padded[..., 1:-1, :-2, :]
    beside = beside + column[..., 2:] + column[..., :-2]
    return inner, beside


def lifted(field):
    return jnp.pad(field, [(0, 0)] * (field.ndim - 1) + [(1, 0)])[..., :-1]


def dropped(field):
    return jnp.pad(field, [(0, 0)] * (field.ndim - 1) + [(0, 1)])[..., 1:]


def base_step(padded, diffusion, courant, uptake):
    inner, beside = spread(padded)
    carried = courant * inner
    return inner + diffusion * (beside - 6.0 * inner) + lifted(carried) - carried - uptake * inner / (HALF_SATURATION + inner)


def tangent_step(padded, diffusion, courant, linear, source):
    inner, beside = spread(padded)
    carried = courant * inner
    return inner + diffusion * (beside - 6.0 * inner) + lifted(carried) - carried - linear * inner - source


def adjoint_step(padded, adjoint, courant, linear):
    inner_q, beside_q = spread(padded)
    return adjoint + beside_q - 6.0 * inner_q + courant * (dropped(adjoint) - adjoint) - linear * adjoint


def reference(conc_start, diffusion, courant, uptake, directions, sensor_cell, sensor_step):
    states = [conc_start]
    current = conc_start
    for step in range(STEPS):
        current = base_step(pad_sides(current), diffusion, courant, uptake)
        states.append(current)
    ratios = [s / (HALF_SATURATION + s) for s in states[:STEPS]]
    linears = [uptake * HALF_SATURATION / ((HALF_SATURATION + s) * (HALF_SATURATION + s)) for s in states[:STEPS]]
    rows_x = sensor_cell // (CY * LZ)
    rows_y = (sensor_cell // LZ) % CY
    layer = sensor_cell % LZ
    base_x = jnp.arange(N_GX, dtype=jnp.int32)[:, None, None] * CX
    base_y = jnp.arange(N_GY, dtype=jnp.int32)[None, :, None] * CY
    cells = (((base_x + rows_x) * NY + base_y + rows_y) * LZ + layer).reshape(-1).astype(jnp.int32)
    when = sensor_step.reshape(-1)

    def single(direction):
        tangent = -(direction * ratios[0])
        observed = []
        for step in range(1, STEPS + 1):
            if step > 1:
                tangent = tangent_step(pad_sides(tangent), diffusion, courant, linears[step - 1], direction * ratios[step - 1])
            values = tangent.reshape(-1)[cells]
            observed.append(jnp.where(when == step, values, jnp.float32(0.0)))
        adjoint = jnp.zeros((NX * NY * LZ,), jnp.float32).at[cells].add(observed[STEPS - 1]).reshape(NX, NY, LZ)
        gradient = jnp.zeros((NX, NY, LZ), jnp.float32)
        for step in range(STEPS - 1, -1, -1):
            gradient = gradient - ratios[step] * adjoint
            if step > 0:
                adjoint = adjoint_step(pad_sides(diffusion * adjoint), adjoint, courant, linears[step])
                adjoint = adjoint.reshape(-1).at[cells].add(observed[step - 1]).reshape(NX, NY, LZ)
        inner, beside = spread(pad_sides(direction))
        return gradient + PRIOR_WEIGHT * ((6.0 + PRIOR_SHIFT) * inner - beside)

    return lax.map(single, directions)
```

```python
import functools

import jax
import jax.numpy as jnp
from jax import lax
from jax.experimental import pallas as pl
from jax.experimental.pallas import tpu as pltpu
from jax.sharding import PartitionSpec as P

STEPS = 4
HALF_SATURATION = 0.5
PRIOR_WEIGHT = 0.2
PRIOR_SHIFT = 0.5
CHUNKS = 2

MESH = pl.DeviceIdType.MESH


def kernel(
    size_x, size_y, groups, depth,
    conc, diffusion, courant, uptake, dirs, cells, when, out,
    vp, t1, t2, t3, q4, q3, q2, a4, a3, a2,
    cbuf, cface, chx, chy,
    d_s, dz_s, b_s, dl_s, dc_s, a_s, r_s, n_s, r0x, r0y,
    c_send, c_recv, f_send, f_recv,
):
    layers = conc.shape[-1]
    ix, iy = lax.axis_index("gx"), lax.axis_index("gy")
    nx, ny = lax.axis_size("gx"), lax.axis_size("gy")
    have = (ix > 0, ix < nx - 1, iy > 0, iy < ny - 1)
    partner = (
        (jnp.maximum(ix - 1, 0), iy),
        (jnp.minimum(ix + 1, nx - 1), iy),
        (ix, jnp.maximum(iy - 1, 0)),
        (ix, jnp.minimum(iy + 1, ny - 1)),
    )
    barrier = pltpu.get_barrier_semaphore()
    for side in range(4):
        @pl.when(have[side])
        def _(side=side):
            pl.semaphore_signal(barrier, inc=1, device_id=partner[side], device_id_type=MESH)

    padded = (vp, t2, t3, q4, q3, q2)

    def halo(buf, g, side):
        if side == 0:
            return buf.at[g, 0, pl.ds(1, size_y)]
        if side == 1:
            return buf.at[g, size_x + 1, pl.ds(1, size_y)]
        if side == 2:
            return buf.at[g, pl.ds(1, size_x), 0]
        return buf.at[g, pl.ds(1, size_x), size_y + 1]

    def face(buf, g, side):
        if side == 0:
            return buf.at[g, 1, pl.ds(1, size_y)]
        if side == 1:
            return buf.at[g, size_x, pl.ds(1, size_y)]
        if side == 2:
            return buf.at[g, pl.ds(1, size_x), 1]
        return buf.at[g, pl.ds(1, size_x), size_y]

    for side in range(4):
        @pl.when(jnp.logical_not(have[side]))
        def _(side=side):
            for step in range(STEPS - 1):
                chx_or_y = chx if side < 2 else chy
                chx_or_y[step, side % 2] = jnp.zeros(chx.shape[2:] if side < 2 else chy.shape[2:], jnp.float32)
            for buf in padded:
                for g in range(groups):
                    ref = halo(buf, g, side)
                    ref[...] = jnp.zeros(ref.shape, jnp.float32)

    @pl.loop(0, size_x)
    def _(x):
        for y in range(size_y):
            for g in range(groups):
                vp[g, x + 1, y + 1] = dirs[
                    pl.ds(g * depth * size_x * size_y + x * size_y + y, depth, stride=size_x * size_y), :
                ]

    c0 = conc[...]
    cbuf[0] = c0

    def rows_of(c, y):
        return jnp.concatenate([c[x, y:y + 1, :] for x in range(size_x)], axis=0)

    cface[0, 0] = rows_of(c0, 0)
    cface[0, 1] = rows_of(c0, size_y - 1)

    pl.semaphore_wait(barrier, sum(jnp.where(side, 1, 0) for side in have))

    def c_copy(step, side):
        other = side ^ 1
        if side < 2:
            src = cbuf.at[step, 0 if side == 0 else size_x - 1]
            dst = chx.at[step, other]
        else:
            src = cface.at[step, side - 2]
            dst = chy.at[step, other - 2]
        return pltpu.make_async_remote_copy(
            src_ref=src, dst_ref=dst, send_sem=c_send.at[step, side], recv_sem=c_recv.at[step, other],
            device_id=partner[side], device_id_type=MESH,
        )

    def c_landed(step, side):
        dst = chx.at[step, side] if side < 2 else chy.at[step, side - 2]
        return pltpu.make_async_remote_copy(
            src_ref=dst, dst_ref=dst, send_sem=c_send.at[step, side], recv_sem=c_recv.at[step, side],
            device_id=partner[side], device_id_type=MESH,
        )

    def f_copy(k, g, side):
        other = side ^ 1
        return pltpu.make_async_remote_copy(
            src_ref=face(padded[k], g, side), dst_ref=halo(padded[k], g, other),
            send_sem=f_send.at[k, g, side], recv_sem=f_recv.at[k, g, other],
            device_id=partner[side], device_id_type=MESH,
        )

    def f_landed(k, g, side):
        dst = halo(padded[k], g, side)
        return pltpu.make_async_remote_copy(
            src_ref=dst, dst_ref=dst, send_sem=f_send.at[k, g, side], recv_sem=f_recv.at[k, g, side],
            device_id=partner[side], device_id_type=MESH,
        )

    def on_sides(action):
        for side in range(4):
            @pl.when(have[side])
            def _(side=side):
                action(side)

    on_sides(lambda side: c_copy(0, side).start())
    for g in range(groups):
        on_sides(lambda side, g=g: f_copy(0, g, side).start())

    layer = lax.broadcasted_iota(jnp.int32, (size_x, size_y, layers), 2)
    first, last = layer == 0, layer == layers - 1
    zero = jnp.zeros((size_x, size_y, layers), jnp.float32)
    d, u, w = diffusion[...], courant[...], uptake[...]

    def lift(f):
        return jnp.where(first, zero, pltpu.roll(f, 1, 2))

    def drop(f):
        return jnp.where(last, zero, pltpu.roll(f, layers - 1, 2))

    d_s[...] = d
    dz_s[...] = jnp.where(last, zero, d)
    b_s[...] = jnp.where(first, zero, d) + lift(u)
    dl_s[...] = lift(d)
    dc_s[...] = drop(d) + jnp.where(last, zero, u)
    r_s[0] = c0 / (HALF_SATURATION + c0)

    cell, time = cells[...], when[...]
    sensors = cell.shape[1]
    column = lax.broadcasted_iota(jnp.int32, (size_x * size_y, sensors), 0)
    depth_of = lax.broadcasted_iota(jnp.int32, (layers, sensors), 0)
    at_layer = jnp.where((cell % layers) == depth_of, jnp.float32(1), jnp.float32(0))
    for step in range(STEPS):
        at_column = jnp.where(
            ((cell // layers) == column) & (time == step + 1), jnp.float32(1), jnp.float32(0)
        )
        n_s[step] = lax.dot_general(
            at_column, at_layer, (((1,), (1,)), ((), ())), preferred_element_type=jnp.float32
        ).reshape(size_x, size_y, layers)

    def next_conc(step):
        on_sides(lambda side: c_landed(step, side).wait_recv())
        c = cbuf[step]
        low_x, high_x = chx[step, 0], chx[step, 1]
        low_y, high_y = chy[step, 0], chy[step, 1]
        xm = jnp.concatenate([low_x[None], c[:-1]], axis=0)
        xp = jnp.concatenate([c[1:], high_x[None]], axis=0)
        row = lax.broadcasted_iota(jnp.int32, (size_x, size_y, layers), 1)
        low_full = jnp.stack([jnp.broadcast_to(low_y[x:x + 1], (size_y, layers)) for x in range(size_x)], axis=0)
        high_full = jnp.stack([jnp.broadcast_to(high_y[x:x + 1], (size_y, layers)) for x in range(size_x)], axis=0)
        ym = jnp.where(row == 0, low_full, pltpu.roll(c, 1, 1))
        yp = jnp.where(row == size_y - 1, high_full, pltpu.roll(c, size_y - 1, 1))
        beside = xm + xp + ym + yp + lift(c) + drop(c)
        carried = u * c
        new = c + d * (beside - 6.0 * c) + lift(carried) - carried - w * c / (HALF_SATURATION + c)
        if step + 1 < STEPS - 1:
            cbuf[step + 1] = new
            cface[step + 1, 0] = rows_of(new, 0)
            cface[step + 1, 1] = rows_of(new, size_y - 1)
            on_sides(lambda side: c_copy(step + 1, side).start())
        held = HALF_SATURATION + new
        r_s[step + 1] = new / held
        a_s[step] = 1.0 - 6.0 * d - u - w * HALF_SATURATION / (held * held)

    def columns(body):
        @pl.loop(0, size_x)
        def _(x):
            for y in range(size_y):
                body(x, y)

    def coef(ref, x, y, *lead):
        return ref[(*lead, x, pl.ds(y, 1), slice(None))]

    def sides_sum(buf, g, x, y):
        return (buf[g, x, y + 1] + buf[g, x + 2, y + 1]) + (buf[g, x + 1, y] + buf[g, x + 1, y + 2])

    def up(f):
        return pltpu.roll(f, 1, 1)

    def down(f):
        return pltpu.roll(f, layers - 1, 1)

    def tangent_at(buf, g, x, y, step):
        p = buf[g, x + 1, y + 1]
        return (
            coef(a_s, x, y, step - 1) * p
            + coef(d_s, x, y) * sides_sum(buf, g, x, y)
            + coef(dz_s, x, y) * down(p)
            + coef(b_s, x, y) * up(p)
            - coef(r_s, x, y, step) * vp[g, x + 1, y + 1]
        )

    def adjoint_at(held, buf, g, x, y, step):
        a = held[g, x, y]
        return (
            coef(a_s, x, y, step - 1) * a
            + sides_sum(buf, g, x, y)
            + coef(dl_s, x, y) * up(a)
            + coef(dc_s, x, y) * down(a)
        )

    for g in range(groups):
        def first_tangent(x, y, g=g):
            t1[g, x + 1, y + 1] = -(vp[g, x + 1, y + 1] * coef(r_s, x, y, 0))
        columns(first_tangent)

    next_conc(0)
    for side in range(2):
        r0x[side] = chx[0, side] / (HALF_SATURATION + chx[0, side])
        r0y[side] = chy[0, side] / (HALF_SATURATION + chy[0, side])

    for g in range(groups):
        on_sides(lambda side, g=g: f_landed(0, g, side).wait_recv())
        for y in range(size_y):
            t1[g, 0, y + 1] = -(vp[g, 0, y + 1] * r0x[0, pl.ds(y, 1), :])
            t1[g, size_x + 1, y + 1] = -(vp[g, size_x + 1, y + 1] * r0x[1, pl.ds(y, 1), :])
        for x in range(size_x):
            t1[g, x + 1, 0] = -(vp[g, x + 1, 0] * r0y[0, pl.ds(x, 1), :])
            t1[g, x + 1, size_y + 1] = -(vp[g, x + 1, size_y + 1] * r0y[1, pl.ds(x, 1), :])

        def second(x, y, g=g):
            t2[g, x + 1, y + 1] = tangent_at(t1, g, x, y, 1)
        columns(second)
        on_sides(lambda side, g=g: f_copy(1, g, side).start())

    next_conc(1)
    for g in range(groups):
        on_sides(lambda side, g=g: f_landed(1, g, side).wait_recv())

        def third(x, y, g=g):
            t3[g, x + 1, y + 1] = tangent_at(t2, g, x, y, 2)
        columns(third)
        on_sides(lambda side, g=g: f_copy(2, g, side).start())

    next_conc(2)
    for g in range(groups):
        on_sides(lambda side, g=g: f_landed(2, g, side).wait_recv())

        def fourth(x, y, g=g):
            a = coef(n_s, x, y, 3) * tangent_at(t3, g, x, y, 3)
            a4[g, x, y] = a
            q4[g, x + 1, y + 1] = coef(d_s, x, y) * a
        columns(fourth)
        on_sides(lambda side, g=g: f_copy(3, g, side).start())

    for g in range(groups):
        on_sides(lambda side, g=g: f_landed(3, g, side).wait_recv())

        def back_three(x, y, g=g):
            a = adjoint_at(a4, q4, g, x, y, 3) + coef(n_s, x, y, 2) * t3[g, x + 1, y + 1]
            a3[g, x, y] = a
            q3[g, x + 1, y + 1] = coef(d_s, x, y) * a
        columns(back_three)
        on_sides(lambda side, g=g: f_copy(4, g, side).start())

    for g in range(groups):
        on_sides(lambda side, g=g: f_landed(4, g, side).wait_recv())

        def back_two(x, y, g=g):
            a = adjoint_at(a3, q3, g, x, y, 2) + coef(n_s, x, y, 1) * t2[g, x + 1, y + 1]
            a2[g, x, y] = a
            q2[g, x + 1, y + 1] = coef(d_s, x, y) * a
        columns(back_two)
        on_sides(lambda side, g=g: f_copy(5, g, side).start())

    lane = lax.broadcasted_iota(jnp.int32, (1, layers), 1)
    not_first = jnp.where(lane == 0, jnp.float32(0), jnp.float32(1))
    not_last = jnp.where(lane == layers - 1, jnp.float32(0), jnp.float32(1))
    for g in range(groups):
        on_sides(lambda side, g=g: f_landed(5, g, side).wait_recv())

        def finish(x, y, g=g):
            a = adjoint_at(a2, q2, g, x, y, 1) + coef(n_s, x, y, 0) * t1[g, x + 1, y + 1]
            gradient = (
                coef(r_s, x, y, 3) * a4[g, x, y]
                + coef(r_s, x, y, 2) * a3[g, x, y]
                + coef(r_s, x, y, 1) * a2[g, x, y]
                + coef(r_s, x, y, 0) * a
            )
            v = vp[g, x + 1, y + 1]
            beside = sides_sum(vp, g, x, y) + not_first * up(v) + not_last * down(v)
            out[
                pl.ds(g * depth * size_x * size_y + x * size_y + y, depth, stride=size_x * size_y), :
            ] = PRIOR_WEIGHT * ((6.0 + PRIOR_SHIFT) * v - beside) - gradient
        columns(finish)

    for step in range(STEPS - 1):
        on_sides(lambda side, step=step: c_copy(step, side).wait_send())
    for k in range(len(padded)):
        for g in range(groups):
            on_sides(lambda side, k=k, g=g: f_copy(k, g, side).wait_send())


def on_device(conc_start, diffusion, courant, uptake, directions, sensor_cell, sensor_step):
    count_dir, size_x, size_y, layers = directions.shape
    groups = CHUNKS
    depth = count_dir // groups
    sensors = sensor_cell.shape[-1]
    vmem = pltpu.VMEM
    pad = vmem((groups, size_x + 2, size_y + 2, depth, layers), jnp.float32)
    own = vmem((groups, size_x, size_y, depth, layers), jnp.float32)
    block = vmem((size_x, size_y, layers), jnp.float32)

    def blocks(n):
        return vmem((n, size_x, size_y, layers), jnp.float32)

    sems = pltpu.SemaphoreType.DMA
    result = pl.pallas_call(
        functools.partial(kernel, size_x, size_y, groups, depth),
        out_shape=jax.ShapeDtypeStruct((count_dir * size_x * size_y, layers), jnp.float32),
        in_specs=[pl.BlockSpec(memory_space=vmem)] * 7,
        out_specs=pl.BlockSpec(memory_space=vmem),
        scratch_shapes=[
            *[pad] * 7,
            *[own] * 3,
            blocks(STEPS - 1),
            vmem((STEPS - 1, 2, size_x, layers), jnp.float32),
            vmem((STEPS - 1, 2, size_y, layers), jnp.float32),
            vmem((STEPS - 1, 2, size_x, layers), jnp.float32),
            *[block] * 5,
            blocks(STEPS - 1),
            blocks(STEPS),
            blocks(STEPS),
            vmem((2, size_y, layers), jnp.float32),
            vmem((2, size_x, layers), jnp.float32),
            sems((STEPS - 1, 4)),
            sems((STEPS - 1, 4)),
            sems((6, groups, 4)),
            sems((6, groups, 4)),
        ],
        compiler_params=pltpu.CompilerParams(collective_id=0, has_side_effects=True),
    )(
        conc_start, diffusion, courant, uptake,
        directions.reshape(count_dir * size_x * size_y, layers),
        sensor_cell.reshape(1, sensors), sensor_step.reshape(1, sensors),
    )
    return result.reshape(count_dir, size_x, size_y, layers)


def solution(mesh):
    in_specs = (
        P("gx", "gy", None),
        P("gx", "gy", None),
        P("gx", "gy", None),
        P("gx", "gy", None),
        P(None, "gx", "gy", None),
        P("gx", "gy", None),
        P("gx", "gy", None),
    )
    out_specs = P(None, "gx", "gy", None)
    return jax.shard_map(
        on_device, mesh=mesh, in_specs=in_specs, out_specs=out_specs, check_vma=False
    )
```

```python
import functools

import jax
import jax.numpy as jnp
from jax import lax
from jax.experimental import pallas as pl
from jax.experimental.pallas import tpu as pltpu
from jax.sharding import PartitionSpec as P

STEPS = 4
HALF_SATURATION = 0.5
PRIOR_WEIGHT = 0.2
PRIOR_SHIFT = 0.5
CHUNKS = 4
NARROW = (2, 3)

MESH = pl.DeviceIdType.MESH


def kernel(
    size_x, size_y, groups, depth,
    conc, diffusion, courant, uptake, dirs, cells, when, out,
    vp, t1, t2, t3, q4, q3, q2, a4, a3, a2,
    cbuf, cface, chx, chy,
    d_s, dz_s, b_s, dl_s, dc_s, a_s, r_s, n_s, r0x, r0y,
    u4, info, info_n, zt, es, er,
    c_send, c_recv, f_send, f_recv, i_send, i_recv, e_send, e_recv,
):
    layers = conc.shape[-1]
    ix, iy = lax.axis_index("gx"), lax.axis_index("gy")
    nx, ny = lax.axis_size("gx"), lax.axis_size("gy")
    have = (ix > 0, ix < nx - 1, iy > 0, iy < ny - 1)
    partner = (
        (jnp.maximum(ix - 1, 0), iy),
        (jnp.minimum(ix + 1, nx - 1), iy),
        (ix, jnp.maximum(iy - 1, 0)),
        (ix, jnp.minimum(iy + 1, ny - 1)),
    )
    barrier = pltpu.get_barrier_semaphore()
    for side in range(4):
        @pl.when(have[side])
        def _(side=side):
            pl.semaphore_signal(barrier, inc=1, device_id=partner[side], device_id_type=MESH)

    padded = (vp, t2, t3, q4, q3, q2)

    def halo(buf, g, side):
        if side == 0:
            return buf.at[g, 0, pl.ds(1, size_y)]
        if side == 1:
            return buf.at[g, size_x + 1, pl.ds(1, size_y)]
        if side == 2:
            return buf.at[g, pl.ds(1, size_x), 0]
        return buf.at[g, pl.ds(1, size_x), size_y + 1]

    def face(buf, g, side):
        if side == 0:
            return buf.at[g, 1, pl.ds(1, size_y)]
        if side == 1:
            return buf.at[g, size_x, pl.ds(1, size_y)]
        if side == 2:
            return buf.at[g, pl.ds(1, size_x), 1]
        return buf.at[g, pl.ds(1, size_x), size_y]

    for side in range(4):
        @pl.when(jnp.logical_not(have[side]))
        def _(side=side):
            for step in range(STEPS - 1):
                chx_or_y = chx if side < 2 else chy
                chx_or_y[step, side % 2] = jnp.zeros(chx.shape[2:] if side < 2 else chy.shape[2:], jnp.float32)
            if side < 2:
                info_n[side] = jnp.zeros(info_n.shape[1:], jnp.int32)
                for k in range(2):
                    for g in range(groups):
                        er[k, g, side] = jnp.zeros(er.shape[3:], jnp.float32)
            for k, buf in enumerate(padded):
                if side < 2 and k in NARROW:
                    continue
                for g in range(groups):
                    ref = halo(buf, g, side)
                    ref[...] = jnp.zeros(ref.shape, jnp.float32)

    @pl.loop(0, size_x)
    def _(x):
        for y in range(size_y):
            for g in range(groups):
                vp[g, x + 1, y + 1] = dirs[
                    pl.ds(g * depth * size_x * size_y + x * size_y + y, depth, stride=size_x * size_y), :
                ]

    for g in range(groups):
        for row in (0, size_x + 1):
            t3[g, row] = jnp.zeros(t3.shape[2:], jnp.float32)
    sensors = cells.shape[1]
    info[...] = jnp.full(info.shape, -1, jnp.int32)
    info[0:1, 0:sensors] = cells[...]
    info[1:2, 0:sensors] = when[...]

    c0 = conc[...]
    cbuf[0] = c0

    def rows_of(c, y):
        return jnp.concatenate([c[x, y:y + 1, :] for x in range(size_x)], axis=0)

    cface[0, 0] = rows_of(c0, 0)
    cface[0, 1] = rows_of(c0, size_y - 1)

    pl.semaphore_wait(barrier, sum(jnp.where(side, 1, 0) for side in have))

    def c_copy(step, side):
        other = side ^ 1
        if side < 2:
            src = cbuf.at[step, 0 if side == 0 else size_x - 1]
            dst = chx.at[step, other]
        else:
            src = cface.at[step, side - 2]
            dst = chy.at[step, other - 2]
        return pltpu.make_async_remote_copy(
            src_ref=src, dst_ref=dst, send_sem=c_send.at[step, side], recv_sem=c_recv.at[step, other],
            device_id=partner[side], device_id_type=MESH,
        )

    def c_landed(step, side):
        dst = chx.at[step, side] if side < 2 else chy.at[step, side - 2]
        return pltpu.make_async_remote_copy(
            src_ref=dst, dst_ref=dst, send_sem=c_send.at[step, side], recv_sem=c_recv.at[step, side],
            device_id=partner[side], device_id_type=MESH,
        )

    def f_copy(k, g, side):
        other = side ^ 1
        return pltpu.make_async_remote_copy(
            src_ref=face(padded[k], g, side), dst_ref=halo(padded[k], g, other),
            send_sem=f_send.at[k, g, side], recv_sem=f_recv.at[k, g, other],
            device_id=partner[side], device_id_type=MESH,
        )

    def f_landed(k, g, side):
        dst = halo(padded[k], g, side)
        return pltpu.make_async_remote_copy(
            src_ref=dst, dst_ref=dst, send_sem=f_send.at[k, g, side], recv_sem=f_recv.at[k, g, side],
            device_id=partner[side], device_id_type=MESH,
        )

    def i_copy(side):
        return pltpu.make_async_remote_copy(
            src_ref=info, dst_ref=info_n.at[side ^ 1], send_sem=i_send.at[side], recv_sem=i_recv.at[side ^ 1],
            device_id=partner[side], device_id_type=MESH,
        )

    def e_copy(k, g, side):
        return pltpu.make_async_remote_copy(
            src_ref=es.at[k, g, side], dst_ref=er.at[k, g, side ^ 1],
            send_sem=e_send.at[k, g, side], recv_sem=e_recv.at[k, g, side ^ 1],
            device_id=partner[side], device_id_type=MESH,
        )

    def e_landed(k, g, side):
        return pltpu.make_async_remote_copy(
            src_ref=er.at[k, g, side], dst_ref=er.at[k, g, side],
            send_sem=e_send.at[k, g, side], recv_sem=e_recv.at[k, g, side],
            device_id=partner[side], device_id_type=MESH,
        )

    def i_landed(side):
        return pltpu.make_async_remote_copy(
            src_ref=info_n.at[side], dst_ref=info_n.at[side], send_sem=i_send.at[side], recv_sem=i_recv.at[side],
            device_id=partner[side], device_id_type=MESH,
        )

    def on_sides(action, sides=(0, 1, 2, 3)):
        for side in sides:
            @pl.when(have[side])
            def _(side=side):
                action(side)

    on_sides(lambda side: c_copy(0, side).start())
    on_sides(lambda side: i_copy(side).start(), (0, 1))
    for g in range(groups):
        on_sides(lambda side, g=g: f_copy(0, g, side).start())

    layer = lax.broadcasted_iota(jnp.int32, (size_x, size_y, layers), 2)
    first, last = layer == 0, layer == layers - 1
    zero = jnp.zeros((size_x, size_y, layers), jnp.float32)
    d, u, w = diffusion[...], courant[...], uptake[...]

    def lift(f):
        return jnp.where(first, zero, pltpu.roll(f, 1, 2))

    def drop(f):
        return jnp.where(last, zero, pltpu.roll(f, layers - 1, 2))

    d_s[...] = d
    dz_s[...] = jnp.where(last, zero, d)
    b_s[...] = jnp.where(first, zero, d) + lift(u)
    dl_s[...] = lift(d)
    dc_s[...] = drop(d) + jnp.where(last, zero, u)
    r_s[0] = c0 / (HALF_SATURATION + c0)

    cell, time = info[0:1], info[1:2]
    sensors = info.shape[1]
    column = lax.broadcasted_iota(jnp.int32, (size_x * size_y, sensors), 0)
    depth_of = lax.broadcasted_iota(jnp.int32, (layers, sensors), 0)
    at_layer = jnp.where((cell % layers) == depth_of, jnp.float32(1), jnp.float32(0))
    zt[2] = at_layer
    for step in range(STEPS):
        at_column = jnp.where(
            ((cell // layers) == column) & (time == step + 1), jnp.float32(1), jnp.float32(0)
        )
        n_s[step] = lax.dot_general(
            at_column, at_layer, (((1,), (1,)), ((), ())), preferred_element_type=jnp.float32
        ).reshape(size_x, size_y, layers)

    def on_face(where, last_face):
        base = (size_x - 1) * size_y if last_face else 0
        col = where[0:1] // layers
        return [
            jnp.where((col == base + y) & (where[1:2] == STEPS), jnp.float32(1), jnp.float32(0))
            for y in range(size_y)
        ]

    def read_face(rows, which, masks):
        read = lax.dot_general(
            jnp.concatenate(rows, axis=0), zt[which], (((1,), (0,)), ((), ())),
            precision=lax.Precision.HIGHEST, preferred_element_type=jnp.float32,
        )
        size = rows[0].shape[0]
        return functools.reduce(
            lambda p, q: p + q, [read[y * size:(y + 1) * size] * masks[y] for y in range(size_y)]
        )

    def place_face(values, which, masks):
        placed = lax.dot_general(
            jnp.concatenate([values * m for m in masks], axis=0), zt[which], (((1,), (1,)), ((), ())),
            precision=lax.Precision.HIGHEST, preferred_element_type=jnp.float32,
        )
        size = values.shape[0]
        return [placed[y * size:(y + 1) * size] for y in range(size_y)]

    def next_conc(step):
        on_sides(lambda side: c_landed(step, side).wait_recv())
        c = cbuf[step]
        low_x, high_x = chx[step, 0], chx[step, 1]
        low_y, high_y = chy[step, 0], chy[step, 1]
        xm = jnp.concatenate([low_x[None], c[:-1]], axis=0)
        xp = jnp.concatenate([c[1:], high_x[None]], axis=0)
        row = lax.broadcasted_iota(jnp.int32, (size_x, size_y, layers), 1)
        low_full = jnp.stack([jnp.broadcast_to(low_y[x:x + 1], (size_y, layers)) for x in range(size_x)], axis=0)
        high_full = jnp.stack([jnp.broadcast_to(high_y[x:x + 1], (size_y, layers)) for x in range(size_x)], axis=0)
        ym = jnp.where(row == 0, low_full, pltpu.roll(c, 1, 1))
        yp = jnp.where(row == size_y - 1, high_full, pltpu.roll(c, size_y - 1, 1))
        beside = xm + xp + ym + yp + lift(c) + drop(c)
        carried = u * c
        new = c + d * (beside - 6.0 * c) + lift(carried) - carried - w * c / (HALF_SATURATION + c)
        if step + 1 < STEPS - 1:
            cbuf[step + 1] = new
            cface[step + 1, 0] = rows_of(new, 0)
            cface[step + 1, 1] = rows_of(new, size_y - 1)
            on_sides(lambda side: c_copy(step + 1, side).start())
        held = HALF_SATURATION + new
        r_s[step + 1] = new / held
        a_s[step] = 1.0 - 6.0 * d - u - w * HALF_SATURATION / (held * held)

    def columns(body):
        @pl.loop(0, size_x)
        def _(x):
            for y in range(size_y):
                body(x, y)

    def coef(ref, x, y, *lead):
        return ref[(*lead, x, pl.ds(y, 1), slice(None))]

    def sides_sum(buf, g, x, y):
        return (buf[g, x, y + 1] + buf[g, x + 2, y + 1]) + (buf[g, x + 1, y] + buf[g, x + 1, y + 2])

    def up(f):
        return pltpu.roll(f, 1, 1)

    def down(f):
        return pltpu.roll(f, layers - 1, 1)

    def tangent_at(buf, g, x, y, step):
        p = buf[g, x + 1, y + 1]
        return (
            coef(a_s, x, y, step - 1) * p
            + coef(d_s, x, y) * sides_sum(buf, g, x, y)
            + coef(dz_s, x, y) * down(p)
            + coef(b_s, x, y) * up(p)
            - coef(r_s, x, y, step) * vp[g, x + 1, y + 1]
        )

    def adjoint_at(held, buf, g, x, y, step):
        a = held[g, x, y]
        return (
            coef(a_s, x, y, step - 1) * a
            + sides_sum(buf, g, x, y)
            + coef(dl_s, x, y) * up(a)
            + coef(dc_s, x, y) * down(a)
        )

    for g in range(groups):
        def first_tangent(x, y, g=g):
            t1[g, x + 1, y + 1] = -(vp[g, x + 1, y + 1] * coef(r_s, x, y, 0))
        columns(first_tangent)

    next_conc(0)
    for side in range(2):
        r0x[side] = chx[0, side] / (HALF_SATURATION + chx[0, side])
        r0y[side] = chy[0, side] / (HALF_SATURATION + chy[0, side])

    for g in range(groups):
        on_sides(lambda side, g=g: f_landed(0, g, side).wait_recv())
        for y in range(size_y):
            t1[g, 0, y + 1] = -(vp[g, 0, y + 1] * r0x[0, pl.ds(y, 1), :])
            t1[g, size_x + 1, y + 1] = -(vp[g, size_x + 1, y + 1] * r0x[1, pl.ds(y, 1), :])
        for x in range(size_x):
            t1[g, x + 1, 0] = -(vp[g, x + 1, 0] * r0y[0, pl.ds(x, 1), :])
            t1[g, x + 1, size_y + 1] = -(vp[g, x + 1, size_y + 1] * r0y[1, pl.ds(x, 1), :])

        def second(x, y, g=g):
            t2[g, x + 1, y + 1] = tangent_at(t1, g, x, y, 1)
        columns(second)
        on_sides(lambda side, g=g: f_copy(1, g, side).start())

    on_sides(lambda side: i_landed(side).wait_recv(), (0, 1))
    for side in range(2):
        zt[side] = jnp.where((info_n[side, 0:1] % layers) == depth_of, jnp.float32(1), jnp.float32(0))
    mine = [on_face(info, side == 1) for side in range(2)]
    theirs = [on_face(info_n.at[side], side == 0) for side in range(2)]
    edge = (0, size_x - 1)
    d_at = [
        read_face([jnp.broadcast_to(coef(d_s, edge[side], y), (8, layers)) for y in range(size_y)], 2, mine[side])[0:1]
        for side in range(2)
    ]

    next_conc(1)
    for g in range(groups):
        on_sides(lambda side, g=g: f_landed(1, g, side).wait_recv())

        def third(x, y, g=g):
            t3[g, x + 1, y + 1] = tangent_at(t2, g, x, y, 2)
        columns(third)
        on_sides(lambda side, g=g: f_copy(2, g, side).start(), (2, 3))
        for side in range(2):
            es[0, g, side] = read_face(
                [t3[g, edge[side] + 1, y + 1] for y in range(size_y)], side, theirs[side]
            )
        on_sides(lambda side, g=g: e_copy(0, g, side).start(), (0, 1))

    next_conc(2)
    for g in range(groups):
        on_sides(lambda side, g=g: f_landed(2, g, side).wait_recv(), (2, 3))

        def fourth(x, y, g=g):
            t4 = tangent_at(t3, g, x, y, 3)
            a = coef(n_s, x, y, 3) * t4
            a4[g, x, y] = a
            q4[g, x + 1, y + 1] = coef(d_s, x, y) * a
            u4[g, x, y] = coef(d_s, x, y) * t4
        columns(fourth)
        on_sides(lambda side, g=g: e_landed(0, g, side).wait_recv(), (0, 1))
        for side in range(2):
            x = edge[side]
            added = er[0, g, side] * d_at[side]
            es[1, g, side] = (
                read_face([u4[g, x, y] for y in range(size_y)], 2, mine[side]) + d_at[side] * added
            )
            for y, more in enumerate(place_face(added, 2, mine[side])):
                a4[g, x, y] = a4[g, x, y] + more
                q4[g, x + 1, y + 1] = q4[g, x + 1, y + 1] + coef(d_s, x, y) * more
        on_sides(lambda side, g=g: e_copy(1, g, side).start(), (0, 1))
        on_sides(lambda side, g=g: f_copy(3, g, side).start(), (2, 3))

    for g in range(groups):
        on_sides(lambda side, g=g: f_landed(3, g, side).wait_recv(), (2, 3))
        on_sides(lambda side, g=g: e_landed(1, g, side).wait_recv(), (0, 1))
        for side in range(2):
            for y, more in enumerate(place_face(er[1, g, side], side, theirs[side])):
                q4[g, 0 if side == 0 else size_x + 1, y + 1] = more

        def back_three(x, y, g=g):
            a = adjoint_at(a4, q4, g, x, y, 3) + coef(n_s, x, y, 2) * t3[g, x + 1, y + 1]
            a3[g, x, y] = a
            q3[g, x + 1, y + 1] = coef(d_s, x, y) * a
        columns(back_three)
        on_sides(lambda side, g=g: f_copy(4, g, side).start())

    for g in range(groups):
        on_sides(lambda side, g=g: f_landed(4, g, side).wait_recv())

        def back_two(x, y, g=g):
            a = adjoint_at(a3, q3, g, x, y, 2) + coef(n_s, x, y, 1) * t2[g, x + 1, y + 1]
            a2[g, x, y] = a
            q2[g, x + 1, y + 1] = coef(d_s, x, y) * a
        columns(back_two)
        on_sides(lambda side, g=g: f_copy(5, g, side).start())

    lane = lax.broadcasted_iota(jnp.int32, (1, layers), 1)
    not_first = jnp.where(lane == 0, jnp.float32(0), jnp.float32(1))
    not_last = jnp.where(lane == layers - 1, jnp.float32(0), jnp.float32(1))
    for g in range(groups):
        on_sides(lambda side, g=g: f_landed(5, g, side).wait_recv())

        def finish(x, y, g=g):
            a = adjoint_at(a2, q2, g, x, y, 1) + coef(n_s, x, y, 0) * t1[g, x + 1, y + 1]
            gradient = (
                coef(r_s, x, y, 3) * a4[g, x, y]
                + coef(r_s, x, y, 2) * a3[g, x, y]
                + coef(r_s, x, y, 1) * a2[g, x, y]
                + coef(r_s, x, y, 0) * a
            )
            v = vp[g, x + 1, y + 1]
            beside = sides_sum(vp, g, x, y) + not_first * up(v) + not_last * down(v)
            out[x * size_y + y, g * depth:(g + 1) * depth] = PRIOR_WEIGHT * ((6.0 + PRIOR_SHIFT) * v - beside) - gradient
        columns(finish)

    for step in range(STEPS - 1):
        on_sides(lambda side, step=step: c_copy(step, side).wait_send())
    for k in range(len(padded)):
        for g in range(groups):
            on_sides(
                lambda side, k=k, g=g: f_copy(k, g, side).wait_send(), (2, 3) if k in NARROW else (0, 1, 2, 3)
            )
    on_sides(lambda side: i_copy(side).wait_send(), (0, 1))
    for k in range(2):
        for g in range(groups):
            on_sides(lambda side, k=k, g=g: e_copy(k, g, side).wait_send(), (0, 1))


def on_device(conc_start, diffusion, courant, uptake, directions, sensor_cell, sensor_step):
    count_dir, size_x, size_y, layers = directions.shape
    groups = CHUNKS
    depth = count_dir // groups
    sensors = sensor_cell.shape[-1]
    lanes = pl.cdiv(sensors, 128) * 128
    vmem = pltpu.VMEM
    pad = vmem((groups, size_x + 2, size_y + 2, depth, layers), jnp.float32)
    own = vmem((groups, size_x, size_y, depth, layers), jnp.float32)
    block = vmem((size_x, size_y, layers), jnp.float32)

    def blocks(n):
        return vmem((n, size_x, size_y, layers), jnp.float32)

    sems = pltpu.SemaphoreType.DMA
    result = pl.pallas_call(
        functools.partial(kernel, size_x, size_y, groups, depth),
        out_shape=jax.ShapeDtypeStruct((size_x * size_y, count_dir, layers), jnp.float32),
        in_specs=[pl.BlockSpec(memory_space=vmem)] * 7,
        out_specs=pl.BlockSpec(memory_space=vmem),
        scratch_shapes=[
            *[pad] * 7,
            *[own] * 3,
            blocks(STEPS - 1),
            vmem((STEPS - 1, 2, size_x, layers), jnp.float32),
            vmem((STEPS - 1, 2, size_y, layers), jnp.float32),
            vmem((STEPS - 1, 2, size_x, layers), jnp.float32),
            *[block] * 5,
            blocks(STEPS - 1),
            blocks(STEPS),
            blocks(STEPS),
            vmem((2, size_y, layers), jnp.float32),
            vmem((2, size_x, layers), jnp.float32),
            own,
            pltpu.VMEM((8, lanes), jnp.int32),
            pltpu.VMEM((2, 8, lanes), jnp.int32),
            vmem((3, layers, lanes), jnp.float32),
            vmem((2, groups, 2, depth, lanes), jnp.float32),
            vmem((2, groups, 2, depth, lanes), jnp.float32),
            sems((STEPS - 1, 4)),
            sems((STEPS - 1, 4)),
            sems((6, groups, 4)),
            sems((6, groups, 4)),
            sems((2,)),
            sems((2,)),
            sems((2, groups, 2)),
            sems((2, groups, 2)),
        ],
        compiler_params=pltpu.CompilerParams(collective_id=0, has_side_effects=True),
    )(
        conc_start, diffusion, courant, uptake,
        directions.reshape(count_dir * size_x * size_y, layers),
        sensor_cell.reshape(1, sensors), sensor_step.reshape(1, sensors),
    )
    return jnp.swapaxes(result, 0, 1).reshape(count_dir, size_x, size_y, layers)


def solution(mesh):
    in_specs = (
        P("gx", "gy", None),
        P("gx", "gy", None),
        P("gx", "gy", None),
        P("gx", "gy", None),
        P(None, "gx", "gy", None),
        P("gx", "gy", None),
        P("gx", "gy", None),
    )
    out_specs = P(None, "gx", "gy", None)
    return jax.shard_map(
        on_device, mesh=mesh, in_specs=in_specs, out_specs=out_specs, check_vma=False
    )
```

```python
import functools

import jax
import jax.numpy as jnp
from jax import lax
from jax.experimental import pallas as pl
from jax.experimental.pallas import tpu as pltpu
from jax.sharding import PartitionSpec as P

STEPS = 4
HALF_SATURATION = 0.5
PRIOR_WEIGHT = 0.2
PRIOR_SHIFT = 0.5
CHUNKS = 4
NARROW = (2, 3)

MESH = pl.DeviceIdType.MESH


def kernel(
    size_x, size_y, groups, depth,
    conc, diffusion, courant, uptake, dirs, cells, when, out,
    vp, t1, t2, t3, q4, q3, q2, a4, a3, a2,
    cbuf, cface, chx, chy,
    d_s, dz_s, b_s, dl_s, dc_s, a_s, r_s, n_s, r0x, r0y,
    u4, info, info_n, zt, es, er,
    c_send, c_recv, f_send, f_recv, i_send, i_recv, e_send, e_recv,
):
    layers = conc.shape[-1]
    ix, iy = lax.axis_index("gx"), lax.axis_index("gy")
    nx, ny = lax.axis_size("gx"), lax.axis_size("gy")
    have = (ix > 0, ix < nx - 1, iy > 0, iy < ny - 1)
    partner = (
        (jnp.maximum(ix - 1, 0), iy),
        (jnp.minimum(ix + 1, nx - 1), iy),
        (ix, jnp.maximum(iy - 1, 0)),
        (ix, jnp.minimum(iy + 1, ny - 1)),
    )
    barrier = pltpu.get_barrier_semaphore()
    for side in range(4):
        @pl.when(have[side])
        def _(side=side):
            pl.semaphore_signal(barrier, inc=1, device_id=partner[side], device_id_type=MESH)

    padded = (vp, t2, t3, q4, q3, q2)

    def halo(buf, g, side):
        if side == 0:
            return buf.at[g, 0, pl.ds(1, size_y)]
        if side == 1:
            return buf.at[g, size_x + 1, pl.ds(1, size_y)]
        if side == 2:
            return buf.at[g, pl.ds(1, size_x), 0]
        return buf.at[g, pl.ds(1, size_x), size_y + 1]

    def face(buf, g, side):
        if side == 0:
            return buf.at[g, 1, pl.ds(1, size_y)]
        if side == 1:
            return buf.at[g, size_x, pl.ds(1, size_y)]
        if side == 2:
            return buf.at[g, pl.ds(1, size_x), 1]
        return buf.at[g, pl.ds(1, size_x), size_y]

    for side in range(4):
        @pl.when(jnp.logical_not(have[side]))
        def _(side=side):
            for step in range(STEPS - 1):
                chx_or_y = chx if side < 2 else chy
                chx_or_y[step, side % 2] = jnp.zeros(chx.shape[2:] if side < 2 else chy.shape[2:], jnp.float32)
            if side < 2:
                info_n[side] = jnp.zeros(info_n.shape[1:], jnp.int32)
                for k in range(2):
                    for g in range(groups):
                        er[k, g, side] = jnp.zeros(er.shape[3:], jnp.float32)
            for k, buf in enumerate(padded):
                if side < 2 and k in NARROW:
                    continue
                for g in range(groups):
                    ref = halo(buf, g, side)
                    ref[...] = jnp.zeros(ref.shape, jnp.float32)

    @pl.loop(0, size_x)
    def _(x):
        for y in range(size_y):
            for g in range(groups):
                vp[g, x + 1, y + 1] = dirs[
                    pl.ds(g * depth * size_x * size_y + x * size_y + y, depth, stride=size_x * size_y), :
                ]

    for g in range(groups):
        for row in (0, size_x + 1):
            t3[g, row] = jnp.zeros(t3.shape[2:], jnp.float32)
    sensors = cells.shape[1]
    info[...] = jnp.full(info.shape, -1, jnp.int32)
    info[0:1, 0:sensors] = cells[...]
    info[1:2, 0:sensors] = when[...]

    c0 = conc[...]
    cbuf[0] = c0

    def rows_of(c, y):
        return jnp.concatenate([c[x, y:y + 1, :] for x in range(size_x)], axis=0)

    cface[0, 0] = rows_of(c0, 0)
    cface[0, 1] = rows_of(c0, size_y - 1)

    pl.semaphore_wait(barrier, sum(jnp.where(side, 1, 0) for side in have))

    def c_copy(step, side):
        other = side ^ 1
        if side < 2:
            src = cbuf.at[step, 0 if side == 0 else size_x - 1]
            dst = chx.at[step, other]
        else:
            src = cface.at[step, side - 2]
            dst = chy.at[step, other - 2]
        return pltpu.make_async_remote_copy(
            src_ref=src, dst_ref=dst, send_sem=c_send.at[step, side], recv_sem=c_recv.at[step, other],
            device_id=partner[side], device_id_type=MESH,
        )

    def c_landed(step, side):
        dst = chx.at[step, side] if side < 2 else chy.at[step, side - 2]
        return pltpu.make_async_remote_copy(
            src_ref=dst, dst_ref=dst, send_sem=c_send.at[step, side], recv_sem=c_recv.at[step, side],
            device_id=partner[side], device_id_type=MESH,
        )

    def f_copy(k, g, side):
        other = side ^ 1
        return pltpu.make_async_remote_copy(
            src_ref=face(padded[k], g, side), dst_ref=halo(padded[k], g, other),
            send_sem=f_send.at[k, g, side], recv_sem=f_recv.at[k, g, other],
            device_id=partner[side], device_id_type=MESH,
        )

    def f_landed(k, g, side):
        dst = halo(padded[k], g, side)
        return pltpu.make_async_remote_copy(
            src_ref=dst, dst_ref=dst, send_sem=f_send.at[k, g, side], recv_sem=f_recv.at[k, g, side],
            device_id=partner[side], device_id_type=MESH,
        )

    def i_copy(side):
        return pltpu.make_async_remote_copy(
            src_ref=info, dst_ref=info_n.at[side ^ 1], send_sem=i_send.at[side], recv_sem=i_recv.at[side ^ 1],
            device_id=partner[side], device_id_type=MESH,
        )

    def e_copy(k, g, side):
        return pltpu.make_async_remote_copy(
            src_ref=es.at[k, g, side], dst_ref=er.at[k, g, side ^ 1],
            send_sem=e_send.at[k, g, side], recv_sem=e_recv.at[k, g, side ^ 1],
            device_id=partner[side], device_id_type=MESH,
        )

    def e_landed(k, g, side):
        return pltpu.make_async_remote_copy(
            src_ref=er.at[k, g, side], dst_ref=er.at[k, g, side],
            send_sem=e_send.at[k, g, side], recv_sem=e_recv.at[k, g, side],
            device_id=partner[side], device_id_type=MESH,
        )

    def i_landed(side):
        return pltpu.make_async_remote_copy(
            src_ref=info_n.at[side], dst_ref=info_n.at[side], send_sem=i_send.at[side], recv_sem=i_recv.at[side],
            device_id=partner[side], device_id_type=MESH,
        )

    def on_sides(action, sides=(0, 1, 2, 3)):
        for side in sides:
            @pl.when(have[side])
            def _(side=side):
                action(side)

    on_sides(lambda side: c_copy(0, side).start())
    on_sides(lambda side: i_copy(side).start(), (0, 1))
    for g in range(groups):
        on_sides(lambda side, g=g: f_copy(0, g, side).start())

    layer = lax.broadcasted_iota(jnp.int32, (size_x, size_y, layers), 2)
    first, last = layer == 0, layer == layers - 1
    zero = jnp.zeros((size_x, size_y, layers), jnp.float32)
    d, u, w = diffusion[...], courant[...], uptake[...]

    def lift(f):
        return jnp.where(first, zero, pltpu.roll(f, 1, 2))

    def drop(f):
        return jnp.where(last, zero, pltpu.roll(f, layers - 1, 2))

    d_s[...] = d
    dz_s[...] = jnp.where(last, zero, d)
    b_s[...] = jnp.where(first, zero, d) + lift(u)
    dl_s[...] = lift(d)
    dc_s[...] = drop(d) + jnp.where(last, zero, u)
    r_s[0] = c0 / (HALF_SATURATION + c0)

    cell, time = info[0:1], info[1:2]
    sensors = info.shape[1]
    column = lax.broadcasted_iota(jnp.int32, (size_x * size_y, sensors), 0)
    depth_of = lax.broadcasted_iota(jnp.int32, (layers, sensors), 0)
    at_layer = jnp.where((cell % layers) == depth_of, jnp.float32(1), jnp.float32(0))
    zt[2] = at_layer
    for step in range(STEPS):
        at_column = jnp.where(
            ((cell // layers) == column) & (time == step + 1), jnp.float32(1), jnp.float32(0)
        )
        n_s[step] = lax.dot_general(
            at_column, at_layer, (((1,), (1,)), ((), ())), preferred_element_type=jnp.float32
        ).reshape(size_x, size_y, layers)

    def on_face(where, last_face):
        base = (size_x - 1) * size_y if last_face else 0
        col = where[0:1] // layers
        return [
            jnp.where((col == base + y) & (where[1:2] == STEPS), jnp.float32(1), jnp.float32(0))
            for y in range(size_y)
        ]

    def read_face(rows, which, masks):
        read = lax.dot_general(
            jnp.concatenate(rows, axis=0), zt[which], (((1,), (0,)), ((), ())),
            precision=lax.Precision.HIGHEST, preferred_element_type=jnp.float32,
        )
        size = rows[0].shape[0]
        return functools.reduce(
            lambda p, q: p + q, [read[y * size:(y + 1) * size] * masks[y] for y in range(size_y)]
        )

    def place_face(values, which, masks):
        placed = lax.dot_general(
            jnp.concatenate([values * m for m in masks], axis=0), zt[which], (((1,), (1,)), ((), ())),
            precision=lax.Precision.HIGHEST, preferred_element_type=jnp.float32,
        )
        size = values.shape[0]
        return [placed[y * size:(y + 1) * size] for y in range(size_y)]

    def next_conc(step):
        on_sides(lambda side: c_landed(step, side).wait_recv())
        c = cbuf[step]
        low_x, high_x = chx[step, 0], chx[step, 1]
        low_y, high_y = chy[step, 0], chy[step, 1]
        xm = jnp.concatenate([low_x[None], c[:-1]], axis=0)
        xp = jnp.concatenate([c[1:], high_x[None]], axis=0)
        row = lax.broadcasted_iota(jnp.int32, (size_x, size_y, layers), 1)
        low_full = jnp.stack([jnp.broadcast_to(low_y[x:x + 1], (size_y, layers)) for x in range(size_x)], axis=0)
        high_full = jnp.stack([jnp.broadcast_to(high_y[x:x + 1], (size_y, layers)) for x in range(size_x)], axis=0)
        ym = jnp.where(row == 0, low_full, pltpu.roll(c, 1, 1))
        yp = jnp.where(row == size_y - 1, high_full, pltpu.roll(c, size_y - 1, 1))
        beside = xm + xp + ym + yp + lift(c) + drop(c)
        carried = u * c
        new = c + d * (beside - 6.0 * c) + lift(carried) - carried - w * c / (HALF_SATURATION + c)
        if step + 1 < STEPS - 1:
            cbuf[step + 1] = new
            cface[step + 1, 0] = rows_of(new, 0)
            cface[step + 1, 1] = rows_of(new, size_y - 1)
            on_sides(lambda side: c_copy(step + 1, side).start())
        held = HALF_SATURATION + new
        r_s[step + 1] = new / held
        a_s[step] = 1.0 - 6.0 * d - u - w * HALF_SATURATION / (held * held)

    def columns(body):
        unroll = 2 if size_x % 2 == 0 else 1

        @pl.loop(0, size_x // unroll)
        def _(pair):
            for part in range(unroll):
                for y in range(size_y):
                    body(pair * unroll + part, y)

    def coef(ref, x, y, *lead):
        return ref[(*lead, x, pl.ds(y, 1), slice(None))]

    def sides_sum(buf, g, x, y):
        return (buf[g, x, y + 1] + buf[g, x + 2, y + 1]) + (buf[g, x + 1, y] + buf[g, x + 1, y + 2])

    def up(f):
        return pltpu.roll(f, 1, 1)

    def down(f):
        return pltpu.roll(f, layers - 1, 1)

    def tangent_at(buf, g, x, y, step):
        p = buf[g, x + 1, y + 1]
        return (
            coef(a_s, x, y, step - 1) * p
            + coef(d_s, x, y) * sides_sum(buf, g, x, y)
            + coef(dz_s, x, y) * down(p)
            + coef(b_s, x, y) * up(p)
            - coef(r_s, x, y, step) * vp[g, x + 1, y + 1]
        )

    def adjoint_at(held, buf, g, x, y, step):
        a = held[g, x, y]
        return (
            coef(a_s, x, y, step - 1) * a
            + sides_sum(buf, g, x, y)
            + coef(dl_s, x, y) * up(a)
            + coef(dc_s, x, y) * down(a)
        )

    for g in range(groups):
        def first_tangent(x, y, g=g):
            t1[g, x + 1, y + 1] = -(vp[g, x + 1, y + 1] * coef(r_s, x, y, 0))
        columns(first_tangent)

    next_conc(0)
    for side in range(2):
        r0x[side] = chx[0, side] / (HALF_SATURATION + chx[0, side])
        r0y[side] = chy[0, side] / (HALF_SATURATION + chy[0, side])

    for g in range(groups):
        on_sides(lambda side, g=g: f_landed(0, g, side).wait_recv())
        for y in range(size_y):
            t1[g, 0, y + 1] = -(vp[g, 0, y + 1] * r0x[0, pl.ds(y, 1), :])
            t1[g, size_x + 1, y + 1] = -(vp[g, size_x + 1, y + 1] * r0x[1, pl.ds(y, 1), :])
        for x in range(size_x):
            t1[g, x + 1, 0] = -(vp[g, x + 1, 0] * r0y[0, pl.ds(x, 1), :])
            t1[g, x + 1, size_y + 1] = -(vp[g, x + 1, size_y + 1] * r0y[1, pl.ds(x, 1), :])

        def second(x, y, g=g):
            t2[g, x + 1, y + 1] = tangent_at(t1, g, x, y, 1)
        columns(second)
        on_sides(lambda side, g=g: f_copy(1, g, side).start())

    on_sides(lambda side: i_landed(side).wait_recv(), (0, 1))
    for side in range(2):
        zt[side] = jnp.where((info_n[side, 0:1] % layers) == depth_of, jnp.float32(1), jnp.float32(0))
    mine = [on_face(info, side == 1) for side in range(2)]
    theirs = [on_face(info_n.at[side], side == 0) for side in range(2)]
    edge = (0, size_x - 1)
    d_at = [
        read_face([jnp.broadcast_to(coef(d_s, edge[side], y), (8, layers)) for y in range(size_y)], 2, mine[side])[0:1]
        for side in range(2)
    ]

    next_conc(1)
    for g in range(groups):
        on_sides(lambda side, g=g: f_landed(1, g, side).wait_recv())

        def third(x, y, g=g):
            t3[g, x + 1, y + 1] = tangent_at(t2, g, x, y, 2)
        columns(third)
        on_sides(lambda side, g=g: f_copy(2, g, side).start(), (2, 3))
        for side in range(2):
            es[0, g, side] = read_face(
                [t3[g, edge[side] + 1, y + 1] for y in range(size_y)], side, theirs[side]
            )
        on_sides(lambda side, g=g: e_copy(0, g, side).start(), (0, 1))

    next_conc(2)
    for g in range(groups):
        on_sides(lambda side, g=g: f_landed(2, g, side).wait_recv(), (2, 3))

        def fourth(x, y, g=g):
            t4 = tangent_at(t3, g, x, y, 3)
            a = coef(n_s, x, y, 3) * t4
            a4[g, x, y] = a
            q4[g, x + 1, y + 1] = coef(d_s, x, y) * a
            u4[g, x, y] = coef(d_s, x, y) * t4
        columns(fourth)
        on_sides(lambda side, g=g: e_landed(0, g, side).wait_recv(), (0, 1))
        for side in range(2):
            x = edge[side]
            added = er[0, g, side] * d_at[side]
            es[1, g, side] = (
                read_face([u4[g, x, y] for y in range(size_y)], 2, mine[side]) + d_at[side] * added
            )
            for y, more in enumerate(place_face(added, 2, mine[side])):
                a4[g, x, y] = a4[g, x, y] + more
                q4[g, x + 1, y + 1] = q4[g, x + 1, y + 1] + coef(d_s, x, y) * more
        on_sides(lambda side, g=g: e_copy(1, g, side).start(), (0, 1))
        on_sides(lambda side, g=g: f_copy(3, g, side).start(), (2, 3))

    for g in range(groups):
        on_sides(lambda side, g=g: f_landed(3, g, side).wait_recv(), (2, 3))
        on_sides(lambda side, g=g: e_landed(1, g, side).wait_recv(), (0, 1))
        for side in range(2):
            for y, more in enumerate(place_face(er[1, g, side], side, theirs[side])):
                q4[g, 0 if side == 0 else size_x + 1, y + 1] = more

        def back_three(x, y, g=g):
            a = adjoint_at(a4, q4, g, x, y, 3) + coef(n_s, x, y, 2) * t3[g, x + 1, y + 1]
            a3[g, x, y] = a
            q3[g, x + 1, y + 1] = coef(d_s, x, y) * a
        columns(back_three)
        on_sides(lambda side, g=g: f_copy(4, g, side).start())

    for g in range(groups):
        on_sides(lambda side, g=g: f_landed(4, g, side).wait_recv())

        def back_two(x, y, g=g):
            a = adjoint_at(a3, q3, g, x, y, 2) + coef(n_s, x, y, 1) * t2[g, x + 1, y + 1]
            a2[g, x, y] = a
            q2[g, x + 1, y + 1] = coef(d_s, x, y) * a
        columns(back_two)
        on_sides(lambda side, g=g: f_copy(5, g, side).start())

    lane = lax.broadcasted_iota(jnp.int32, (1, layers), 1)
    not_first = jnp.where(lane == 0, jnp.float32(0), jnp.float32(1))
    not_last = jnp.where(lane == layers - 1, jnp.float32(0), jnp.float32(1))
    for g in range(groups):
        on_sides(lambda side, g=g: f_landed(5, g, side).wait_recv())

        def finish(x, y, g=g):
            a = adjoint_at(a2, q2, g, x, y, 1) + coef(n_s, x, y, 0) * t1[g, x + 1, y + 1]
            gradient = (
                coef(r_s, x, y, 3) * a4[g, x, y]
                + coef(r_s, x, y, 2) * a3[g, x, y]
                + coef(r_s, x, y, 1) * a2[g, x, y]
                + coef(r_s, x, y, 0) * a
            )
            v = vp[g, x + 1, y + 1]
            beside = sides_sum(vp, g, x, y) + not_first * up(v) + not_last * down(v)
            out[x * size_y + y, g * depth:(g + 1) * depth] = PRIOR_WEIGHT * ((6.0 + PRIOR_SHIFT) * v - beside) - gradient
        columns(finish)

    for step in range(STEPS - 1):
        on_sides(lambda side, step=step: c_copy(step, side).wait_send())
    for k in range(len(padded)):
        for g in range(groups):
            on_sides(
                lambda side, k=k, g=g: f_copy(k, g, side).wait_send(), (2, 3) if k in NARROW else (0, 1, 2, 3)
            )
    on_sides(lambda side: i_copy(side).wait_send(), (0, 1))
    for k in range(2):
        for g in range(groups):
            on_sides(lambda side, k=k, g=g: e_copy(k, g, side).wait_send(), (0, 1))


def on_device(conc_start, diffusion, courant, uptake, directions, sensor_cell, sensor_step):
    count_dir, size_x, size_y, layers = directions.shape
    groups = CHUNKS
    depth = count_dir // groups
    sensors = sensor_cell.shape[-1]
    lanes = pl.cdiv(sensors, 128) * 128
    vmem = pltpu.VMEM
    pad = vmem((groups, size_x + 2, size_y + 2, depth, layers), jnp.float32)
    own = vmem((groups, size_x, size_y, depth, layers), jnp.float32)
    block = vmem((size_x, size_y, layers), jnp.float32)

    def blocks(n):
        return vmem((n, size_x, size_y, layers), jnp.float32)

    sems = pltpu.SemaphoreType.DMA
    result = pl.pallas_call(
        functools.partial(kernel, size_x, size_y, groups, depth),
        out_shape=jax.ShapeDtypeStruct((size_x * size_y, count_dir, layers), jnp.float32),
        in_specs=[pl.BlockSpec(memory_space=vmem)] * 7,
        out_specs=pl.BlockSpec(memory_space=vmem),
        scratch_shapes=[
            *[pad] * 7,
            *[own] * 3,
            blocks(STEPS - 1),
            vmem((STEPS - 1, 2, size_x, layers), jnp.float32),
            vmem((STEPS - 1, 2, size_y, layers), jnp.float32),
            vmem((STEPS - 1, 2, size_x, layers), jnp.float32),
            *[block] * 5,
            blocks(STEPS - 1),
            blocks(STEPS),
            blocks(STEPS),
            vmem((2, size_y, layers), jnp.float32),
            vmem((2, size_x, layers), jnp.float32),
            own,
            pltpu.VMEM((8, lanes), jnp.int32),
            pltpu.VMEM((2, 8, lanes), jnp.int32),
            vmem((3, layers, lanes), jnp.float32),
            vmem((2, groups, 2, depth, lanes), jnp.float32),
            vmem((2, groups, 2, depth, lanes), jnp.float32),
            sems((STEPS - 1, 4)),
            sems((STEPS - 1, 4)),
            sems((6, groups, 4)),
            sems((6, groups, 4)),
            sems((2,)),
            sems((2,)),
            sems((2, groups, 2)),
            sems((2, groups, 2)),
        ],
        compiler_params=pltpu.CompilerParams(collective_id=0, has_side_effects=True),
    )(
        conc_start, diffusion, courant, uptake,
        directions.reshape(count_dir * size_x * size_y, layers),
        sensor_cell.reshape(1, sensors), sensor_step.reshape(1, sensors),
    )
    return jnp.swapaxes(result, 0, 1).reshape(count_dir, size_x, size_y, layers)


def solution(mesh):
    in_specs = (
        P("gx", "gy", None),
        P("gx", "gy", None),
        P("gx", "gy", None),
        P("gx", "gy", None),
        P(None, "gx", "gy", None),
        P("gx", "gy", None),
        P("gx", "gy", None),
    )
    out_specs = P(None, "gx", "gy", None)
    return jax.shard_map(
        on_device, mesh=mesh, in_specs=in_specs, out_specs=out_specs, check_vma=False
    )
```
